128 devices in a mesh: pts: 8 (over x, core), snap: 16 (over z, y).
Axes of the slice: x: 4, y: 4, z: 4, core: 2. Of those that a mesh axis runs over, the one named last changes fastest.
Arguments:
- snapshots: bfloat16 [1024, 3, 65536], P('snap', None, 'pts')
- block_starts: int32 [31], replicated, may hold values from 0 to 960, as said below
- point_slab: int32 [65536], P(('pts', 'snap')), may hold values from 0 to 15
- slab_weight: float32 [16], replicated, may hold values from 1 to 10
Outputs:
- mode_field: bfloat16 [2, 33, 31, 3, 65536], P(None, None, None, None, ('pts', 'snap'))
- r_factor: float32 [2, 33, 31, 31], replicated
The draws below stay inside these ranges and needn't reach their ends.
Inputs may be any that keep to these rules, and one draw needn't show every extreme that they name: `block_starts`: strictly increasing; the first is 0 and the last is 960; neighbours lie more than 16 apart.
All inputs are finite; a program needn't handle non-finite values.
Results may differ from the reference program's by a relative error of at most 0.0017.
The reference program's roundings to bfloat16 on the way (of `dft_table`) count: a program that leaves them out, or rounds other values in their place, can miss the bound.
Values may be sent and summed in bfloat16 or wider, within the bound.
No kernel may reach another device: no remote copies, remote signals or barrier semaphores. Data moves between devices by JAX's collectives and lax.ppermute only.
A program may use at most 128 MiB of HBM per device.

```python
import math
import jax
import jax.numpy as jnp
from jax import lax

NT = 1024
WIN = 64
NSLAB = 16
HOP = 32
NB = 31
NF = 33
NP = 65536


def draw_snapshots(key, part):
    position = jnp.arange(NP, dtype=jnp.float32) / NP
    time_index = jnp.arange(NT, dtype=jnp.int32)
    top_bits = NT.bit_length() - 1
    noise_key = jax.random.fold_in(key, 11)
    values = 0.6 * jnp.clip(jax.random.normal(noise_key, (NT, 3, NP), jnp.float32), -6.0, 6.0)
    envelope = jnp.exp(0.5 * jnp.log(3.0) * position)
    for wave_index in range(8):
        wave_key = jax.random.fold_in(key, 100 + wave_index)
        key_bits, key_cycle, key_cos, key_sin = jax.random.split(wave_key, 4)
        bit_count = jax.random.randint(key_bits, (), 2, top_bits, dtype=jnp.int32)
        cycle_top = jnp.left_shift(jnp.int32(1), bit_count)
        cycle_count = jax.random.randint(key_cycle, (), 1, cycle_top, dtype=jnp.int32)
        phase_index = cycle_count * time_index % NT
        phase_angle = 2.0 * math.pi / NT * phase_index.astype(jnp.float32)
        bin_value = cycle_count.astype(jnp.float32) * (WIN / NT)
        strength = 1.2 / jnp.sqrt(1.0 + bin_value)
        coef_cos = jax.random.normal(key_cos, (3, NP), jnp.float32)
        coef_sin = jax.random.normal(key_sin, (3, NP), jnp.float32)
        values = values + strength * (jnp.cos(phase_angle)[:, None, None] * coef_cos[None] + jnp.sin(phase_angle)[:, None, None] * coef_sin[None])
    return (values * envelope[None, None, :]).astype(jnp.bfloat16)


def draw_block_starts(key, part):
    index = jnp.arange(NB, dtype=jnp.int32)
    jitter = jax.random.randint(key, (NB,), 0, HOP // 2, dtype=jnp.int32)
    inner = (index > 0) & (index < NB - 1)
    return index * HOP + jnp.where(inner, jitter, jnp.zeros_like(jitter))


def set_ends(array, own_key, low, top_value):
    longest = array.shape.index(max(array.shape))
    spots = []
    for shift in (0, 1):
        where = [jax.random.randint(jax.random.fold_in(own_key, axis), (), 0, length) for axis, length in enumerate(array.shape)]
        where[longest] = (where[longest] + shift) % array.shape[longest]
        spots.append(tuple(where))
    return array.at[spots[0]].set(low).at[spots[1]].set(top_value)


def setup_inputs(seed: int = 0) -> dict:
    splits = jax.random.split(jax.random.key(seed), 5)
    snapshots = draw_snapshots(jax.random.fold_in(splits[4], 71), 0)
    block_starts = draw_block_starts(jax.random.fold_in(splits[4], 71), 0)
    point_slab = set_ends(jax.random.randint(splits[2], (NP,), 0, NSLAB), jax.random.fold_in(splits[2], 1), 0, NSLAB - 1).astype(jnp.int32)
    slab_weight = jnp.clip(jnp.exp(jax.random.uniform(splits[3], (NSLAB,), jnp.float32, math.log(1.0), math.log(10.0))), 1.0, 10.0)
    return dict(snapshots=snapshots, block_starts=block_starts, point_slab=point_slab, slab_weight=slab_weight)


def make_tables(length, freq_count):
    steps_time = jnp.arange(length, dtype=jnp.int32)
    freq_index = jnp.arange(freq_count, dtype=jnp.int32)
    phase_index = freq_index[:, None] * steps_time[None, :] % length
    angle_value = 2.0 * math.pi / length * phase_index.astype(jnp.float32)
    window = 0.5 - 0.5 * jnp.cos(2.0 * math.pi / length * steps_time.astype(jnp.float32))
    dft_table = jnp.stack([window[None, :] * jnp.cos(angle_value), -window[None, :] * jnp.sin(angle_value)]).astype(jnp.bfloat16)
    row_sums = lax.optimization_barrier(jnp.sum(dft_table.astype(jnp.float32), axis=2))
    return (dft_table, row_sums)

def spectra(series, starts, dft_table, row_sums):
    blocks = jax.vmap(lambda offset: lax.dynamic_slice_in_dim(series, offset, WIN, 0))(starts)
    raw_spec = jnp.einsum('kfw,bwcp->kfbcp', dft_table.astype(jnp.float32), blocks.astype(jnp.float32), precision=lax.Precision.HIGHEST)
    time_mean = lax.optimization_barrier(jnp.sum(series.astype(jnp.float32), axis=0)) / NT
    return raw_spec - row_sums[:, :, None, None, None] * time_mean[None, None, None]

def gram(amplitude):
    highest = lax.Precision.HIGHEST
    amp_real, amp_imag = (amplitude[0], amplitude[1])
    part_real = jnp.einsum('fbn,fdn->bdf', amp_real, amp_real, precision=highest) + jnp.einsum('fbn,fdn->bdf', amp_imag, amp_imag, precision=highest)
    part_imag = jnp.einsum('fbn,fdn->bdf', amp_real, amp_imag, precision=highest) - jnp.einsum('fbn,fdn->bdf', amp_imag, amp_real, precision=highest)
    return (part_real, part_imag)

def complex_cholesky(gram_real, gram_imag):
    size_n = gram_real.shape[0]
    positions = jnp.arange(size_n, dtype=jnp.int32)
    rows_real = []
    rows_imag = []
    for column in range(size_n):
        rest_real = gram_real[column]
        rest_imag = gram_imag[column]
        if column > 0:
            done_real = jnp.stack(rows_real)
            done_imag = jnp.stack(rows_imag)
            above_real = done_real[:, column]
            above_imag = done_imag[:, column]
            rest_real = rest_real - lax.optimization_barrier(jnp.sum(above_real[:, None] * done_real + above_imag[:, None] * done_imag, axis=0))
            rest_imag = rest_imag - lax.optimization_barrier(jnp.sum(above_real[:, None] * done_imag - above_imag[:, None] * done_real, axis=0))
        pivot_value = jnp.sqrt(rest_real[column])
        keep_real = (positions >= column)[:, None]
        keep_imag = (positions > column)[:, None]
        rows_real.append(jnp.where(keep_real, rest_real / pivot_value, jnp.zeros_like(rest_real)))
        rows_imag.append(jnp.where(keep_imag, rest_imag / pivot_value, jnp.zeros_like(rest_imag)))
    return (jnp.stack(rows_real), jnp.stack(rows_imag))

def upper_inverse(upper_real, upper_imag):
    size_n = upper_real.shape[0]
    identity = jnp.eye(size_n, dtype=upper_real.dtype)
    rows_real = []
    rows_imag = []
    for row_index in reversed(range(size_n)):
        rest_real = jnp.broadcast_to(identity[row_index][:, None], upper_real.shape[1:])
        rest_imag = jnp.zeros_like(rest_real)
        if row_index < size_n - 1:
            done_real = jnp.stack(rows_real[::-1])
            done_imag = jnp.stack(rows_imag[::-1])
            coef_real = upper_real[row_index, row_index + 1:]
            coef_imag = upper_imag[row_index, row_index + 1:]
            rest_real = rest_real - lax.optimization_barrier(jnp.sum(coef_real[:, None] * done_real - coef_imag[:, None] * done_imag, axis=0))
            rest_imag = rest_imag - lax.optimization_barrier(jnp.sum(coef_real[:, None] * done_imag + coef_imag[:, None] * done_real, axis=0))
        pivot_value = upper_real[row_index, row_index]
        rows_real.append(rest_real / pivot_value)
        rows_imag.append(rest_imag / pivot_value)
    return (jnp.stack(rows_real[::-1]), jnp.stack(rows_imag[::-1]))

def project(amplitude, inv_real, inv_imag):
    highest = lax.Precision.HIGHEST
    amp_real, amp_imag = (amplitude[0], amplitude[1])
    mode_real = jnp.einsum('fbn,bmf->fmn', amp_real, inv_real, precision=highest) - jnp.einsum('fbn,bmf->fmn', amp_imag, inv_imag, precision=highest)
    mode_imag = jnp.einsum('fbn,bmf->fmn', amp_real, inv_imag, precision=highest) + jnp.einsum('fbn,bmf->fmn', amp_imag, inv_real, precision=highest)
    return jnp.stack([mode_real, mode_imag])

def reference(snapshots, block_starts, point_slab, slab_weight):
    all_points = snapshots.shape[2]
    piece_size = min(all_points, 4096)
    piece_count = all_points // piece_size
    dft_table, row_sums = make_tables(WIN, NF)
    weights = slab_weight[point_slab]
    root_weight = jnp.sqrt(weights / (0.375 * WIN)).reshape(piece_count, piece_size)
    pieces = jnp.moveaxis(snapshots.reshape(NT, 3, piece_count, piece_size), 2, 0)

    def amplitude_of(series, root_piece):
        spectrum = spectra(series, block_starts, dft_table, row_sums)
        return (spectrum * root_piece).reshape(2, NF, NB, 3 * piece_size)

    def piece_gram(inputs):
        return gram(amplitude_of(inputs[0], inputs[1]))
    sums_real, sums_imag = lax.map(piece_gram, (pieces, root_weight))
    norm_scale = 1.0 / (3.0 * all_points)
    gram_real = lax.optimization_barrier(jnp.sum(sums_real, axis=0)) * norm_scale
    gram_imag = lax.optimization_barrier(jnp.sum(sums_imag, axis=0)) * norm_scale
    upper_real, upper_imag = complex_cholesky(gram_real, gram_imag)
    inv_real, inv_imag = upper_inverse(upper_real, upper_imag)

    def piece_modes(inputs):
        amplitude = amplitude_of(inputs[0], inputs[1])
        return project(amplitude, inv_real, inv_imag).reshape(2, NF, NB, 3, piece_size).astype(jnp.bfloat16)
    modes = lax.map(piece_modes, (pieces, root_weight))
    mode_field = jnp.moveaxis(modes, 0, 4).reshape(2, NF, NB, 3, all_points)
    r_factor = jnp.transpose(jnp.stack([upper_real, upper_imag]), (0, 3, 1, 2))
    return (mode_field, r_factor)
```

```python
import functools
import math

import jax
import jax.numpy as jnp
import numpy as np
from jax import lax
from jax.experimental import pallas as pl
from jax.experimental.pallas import tpu as pltpu
from jax.sharding import PartitionSpec as P

NT = 1024
WIN = 64
NF = WIN // 2 + 1
NB = 31
PAD = 32
GROUPS = 9
PACK = 4
MIB = 1 << 20


def make_tables(length, freq_count):
    steps_time = jnp.arange(length, dtype=jnp.int32)
    freq_index = jnp.arange(freq_count, dtype=jnp.int32)
    phase_index = freq_index[:, None] * steps_time[None, :] % length
    angle_value = 2.0 * math.pi / length * phase_index.astype(jnp.float32)
    window = 0.5 - 0.5 * jnp.cos(2.0 * math.pi / length * steps_time.astype(jnp.float32))
    dft_table = jnp.stack(
        [window[None, :] * jnp.cos(angle_value), -window[None, :] * jnp.sin(angle_value)]
    ).astype(jnp.bfloat16)
    row_sums = jnp.sum(dft_table.astype(jnp.float32), axis=2)
    return (dft_table, row_sums)


def pack_kernel(x_ref, o_ref):
    o_ref[0] = x_ref[...]


def pack(x, parts):
    comps, steps, width = x.shape
    piece = width // parts
    return pl.pallas_call(
        pack_kernel,
        grid=(parts,),
        in_specs=[pl.BlockSpec((comps, steps, piece), lambda i: (0, 0, i))],
        out_specs=pl.BlockSpec((1, comps, steps, piece), lambda i: (i, 0, 0, 0)),
        out_shape=jax.ShapeDtypeStruct((parts, comps, steps, piece), x.dtype),
        name="pack",
    )(x)


def shift_kernel(starts_ref, table_ref, d_ref):
    steps = lax.broadcasted_iota(jnp.int32, (PAD, NT), 1)
    offset = steps - starts_ref[...]
    index = jnp.where((offset >= 0) & (offset < WIN), offset, WIN)

    def body(f, carry):
        for k in range(2):
            row = jnp.broadcast_to(table_ref[pl.ds(2 * f + k, 1), :], (PAD, 128))
            for tile in range(NT // 128):
                part = index[:, tile * 128 : (tile + 1) * 128]
                value = jnp.take_along_axis(row, part, axis=1, mode="promise_in_bounds")
                d_ref[pl.ds(pl.multiple_of(f * 64 + k * PAD, PAD), PAD), tile * 128 : (tile + 1) * 128] = value.astype(jnp.bfloat16)
        return carry

    lax.fori_loop(0, NF, body, 0)


def shifted_tables(starts, table):
    starts_col = jnp.broadcast_to(
        jnp.concatenate([starts, jnp.full((1,), 2 * NT, jnp.int32)])[:, None], (PAD, NT)
    )
    rows = jnp.zeros((NF * 2, 128), jnp.float32).at[:, :WIN].set(
        jnp.transpose(table, (1, 0, 2)).reshape(NF * 2, WIN).astype(jnp.float32)
    )
    return pl.pallas_call(
        shift_kernel,
        out_shape=jax.ShapeDtypeStruct((NF * 64, NT), jnp.bfloat16),
        compiler_params=pltpu.CompilerParams(vmem_limit_bytes=32 * MIB),
        name="shift_tables",
    )(starts_col, rows)


def spectra_kernel(sums_ref, d_ref, x_ref, root_ref, a_ref, g_ref, s_ref, acc_ref):
    comp = pl.program_id(0)
    series = x_ref[...].reshape(NT, x_ref.shape[3])
    mean = jnp.sum(series.astype(jnp.float32), axis=0, keepdims=True) / NT
    root = root_ref[...]

    @pl.when(comp == 0)
    def _():
        acc_ref[...] = jnp.zeros_like(acc_ref)

    rows = 11 * 64

    def product(i, carry):
        at = pl.ds(pl.multiple_of(i * rows, rows), rows)
        s_ref[at, :] = jnp.dot(d_ref[at, :], series, preferred_element_type=jnp.float32)
        return carry

    lax.fori_loop(0, NF // 11, product, 0)

    def one(f, carry):
        top = s_ref[pl.ds(pl.multiple_of(f * 64, 64), PAD), :]
        low = s_ref[pl.ds(pl.multiple_of(f * 64 + PAD, PAD), PAD), :]
        top = (top - sums_ref[2 * f] * mean) * root
        low = (low - sums_ref[2 * f + 1] * mean) * root
        amp = jnp.concatenate([top, low], axis=0)
        high = amp.astype(jnp.bfloat16)
        rest = (amp - high.astype(jnp.float32)).astype(jnp.bfloat16)
        both = jnp.concatenate([high, rest], axis=0)
        a_ref[0, f] = both
        acc_ref[f] += lax.dot_general(
            both, both, (((1,), (1,)), ((), ())), preferred_element_type=jnp.float32
        )
        return carry

    lax.fori_loop(0, NF, one, 0)

    @pl.when(comp == pl.num_programs(0) - 1)
    def _():
        row = lax.broadcasted_iota(jnp.int32, (PAD, 128), 0)
        lane = lax.broadcasted_iota(jnp.int32, (PAD, 128), 1)

        def packed(f):
            quad = acc_ref[f]
            half = quad[:64] + quad[64:]
            full = half + pltpu.roll(half, 64, 1)
            real = full[:PAD] + pltpu.roll(full[PAD:], 96, 1)
            imag = pltpu.roll(full[:PAD], 96, 1) - full[PAD:]
            return jnp.where(lane < PAD, jnp.where(row <= lane, real, imag), 0.0)

        def group(g, carry):
            total = packed(PACK * g)
            for q in range(1, PACK):
                total = total + pltpu.roll(packed(PACK * g + q), PAD * q, 1)
            g_ref[g] = total
            return carry

        lax.fori_loop(0, GROUPS - 1, group, 0)
        g_ref[GROUPS - 1] = packed(NF - 1)


def spectra_and_gram(sums, tables, series, root):
    parts, comps, steps, width = series.shape
    return pl.pallas_call(
        spectra_kernel,
        grid=(comps,),
        in_specs=[
            pl.BlockSpec(memory_space=pltpu.SMEM),
            pl.BlockSpec((NF * 64, NT), lambda c: (0, 0), pipeline_mode=pl.Buffered(1)),
            pl.BlockSpec((parts, 1, steps, width), lambda c: (0, c, 0, 0)),
            pl.BlockSpec((1, width), lambda c: (0, 0)),
        ],
        out_specs=[
            pl.BlockSpec((1, NF, 128, width), lambda c: (c, 0, 0, 0)),
            pl.BlockSpec((GROUPS, PAD, 128), lambda c: (0, 0, 0)),
        ],
        out_shape=[
            jax.ShapeDtypeStruct((comps, NF, 128, width), jnp.bfloat16),
            jax.ShapeDtypeStruct((GROUPS, PAD, 128), jnp.float32),
        ],
        scratch_shapes=[
            pltpu.VMEM((NF * 64, width), jnp.float32),
            pltpu.VMEM((NF, 128, 128), jnp.float32),
        ],
        compiler_params=pltpu.CompilerParams(vmem_limit_bytes=48 * MIB),
        name="spectra_gram",
    )(sums, tables, series, root)


def factor_kernel(scale, m_ref, w_ref, r_ref, gr_ref, gi_ref, lr_ref, li_ref, mix_ref):
    row = lax.broadcasted_iota(jnp.int32, (PAD, 128), 0)
    lane = lax.broadcasted_iota(jnp.int32, (PAD, 128), 1)
    col = lane % PAD
    block = lane // PAD
    eye = (col == row).astype(jnp.float32)

    for g in range(GROUPS):
        packed = m_ref[g] * scale
        turned = jnp.transpose(jnp.concatenate([packed] * PACK, axis=0))
        other = jnp.where(block == 0, turned[:PAD], 0.0)
        for q in range(1, PACK):
            other = jnp.where(block == q, turned[q * PAD : (q + 1) * PAD], other)
        real = jnp.where(col >= row, packed, other)
        imag = jnp.where(col < row, packed, jnp.where(col > row, -other, 0.0))
        spare = PACK * g + block >= NF
        gr_ref[g] = jnp.where(spare, eye, real)
        gi_ref[g] = jnp.where(spare, 0.0, imag)
        lr_ref[g] = eye
        li_ref[g] = jnp.zeros_like(eye)

    def pick(x, index):
        return jnp.take_along_axis(x, index, axis=1, mode="promise_in_bounds")

    def column(j, carry):
        index = block * PAD + j
        below = row > j
        for g in range(GROUPS):
            real, imag = gr_ref[g], gi_ref[g]
            at = pl.ds(j, 1)
            row_real, row_imag = gr_ref[g, at, :], gi_ref[g, at, :]
            low_real, low_imag = lr_ref[g, at, :], li_ref[g, at, :]
            pivot = pick(jnp.broadcast_to(row_real, (8, 128)), index[:8])[:1]
            inverse = 1.0 / pivot
            mult_real = jnp.where(below, pick(real, index) * inverse, 0.0)
            mult_imag = jnp.where(below, pick(imag, index) * inverse, 0.0)
            gr_ref[g] = real - (mult_real * row_real - mult_imag * row_imag)
            gi_ref[g] = imag - (mult_real * row_imag + mult_imag * row_real)
            lr_ref[g] = lr_ref[g] - (mult_real * low_real - mult_imag * low_imag)
            li_ref[g] = li_ref[g] - (mult_real * low_imag + mult_imag * low_real)
        return carry

    lax.fori_loop(0, NB, column, 0)

    for g in range(GROUPS):
        pivot = pick(gr_ref[g], block * PAD + row)
        root = 1.0 / jnp.sqrt(pivot)
        r_ref[0, g] = jnp.where(col >= row, gr_ref[g] * root, 0.0)
        r_ref[1, g] = jnp.where(col > row, gi_ref[g] * root, 0.0)
        low_real = lr_ref[g] * root
        low_imag = li_ref[g] * root
        for q in range(PACK):
            if PACK * g + q >= NF:
                continue
            real = pltpu.roll(low_real, (128 - PAD * q) % 128, 1)
            imag = pltpu.roll(low_imag, (128 - PAD * q) % 128, 1)
            real_next = pltpu.roll(low_real, (160 - PAD * q) % 128, 1)
            imag_next = pltpu.roll(low_imag, (160 - PAD * q) % 128, 1)
            first = jnp.where(lane < PAD, real, imag_next)
            second = jnp.where(lane < PAD, -imag, real_next)
            mix_ref[pl.ds(0, PAD, stride=2), :] = jnp.where(lane < 64, first, 0.0)
            mix_ref[pl.ds(1, PAD, stride=2), :] = jnp.where(lane < 64, second, 0.0)
            full = mix_ref[...]
            high = full.astype(jnp.bfloat16).astype(jnp.float32)
            rest = full - high
            both = jnp.concatenate(
                [high + pltpu.roll(high, 64, 1), rest + pltpu.roll(rest, 64, 1)], axis=0
            )
            w_ref[PACK * g + q] = both.astype(jnp.bfloat16)


def factor(gram, scale):
    return pl.pallas_call(
        functools.partial(factor_kernel, scale),
        out_shape=[
            jax.ShapeDtypeStruct((NF, 128, 128), jnp.bfloat16),
            jax.ShapeDtypeStruct((2, GROUPS, PAD, 128), jnp.float32),
        ],
        scratch_shapes=[pltpu.VMEM((GROUPS, PAD, 128), jnp.float32)] * 4
        + [pltpu.VMEM((64, 128), jnp.float32)],
        compiler_params=pltpu.CompilerParams(vmem_limit_bytes=32 * MIB),
        name="factor",
    )(gram)


def project_kernel(w_ref, a_ref, o_ref):
    for c in range(a_ref.shape[0]):
        out = jnp.dot(w_ref[0], a_ref[c, 0], preferred_element_type=jnp.float32)
        mode = (out[:64] + out[64:]).astype(jnp.bfloat16)
        o_ref[0, :, c] = mode.reshape(PAD, 2, mode.shape[1])[:NB]


def project(weights, amplitude):
    comps, freqs, rows, width = amplitude.shape
    return pl.pallas_call(
        project_kernel,
        grid=(freqs,),
        in_specs=[
            pl.BlockSpec((1, 128, 128), lambda f: (f, 0, 0)),
            pl.BlockSpec((comps, 1, rows, width), lambda f: (0, f, 0, 0)),
        ],
        out_specs=pl.BlockSpec((1, NB, comps, 2, width), lambda f: (f, 0, 0, 0, 0)),
        out_shape=jax.ShapeDtypeStruct((freqs, NB, comps, 2, width), jnp.bfloat16),
        compiler_params=pltpu.CompilerParams(vmem_limit_bytes=32 * MIB),
        name="project",
    )(weights, amplitude)


def sum_everywhere(x):
    both = ("pts", "snap")
    snap = lax.axis_size("snap")
    count = lax.axis_size("pts") * snap

    def swap(value, mask):
        return lax.ppermute(value, both, [(i, i ^ mask) for i in range(count)])

    half = x.shape[0] // 2
    core = lax.axis_index("pts") % 2
    mine = jnp.where(core == 0, x[:half], x[half:])
    other = jnp.where(core == 0, x[half:], x[:half])
    total = mine + swap(other, snap)
    mask = 1
    while mask < count:
        if mask != snap:
            total = total + swap(total, mask)
        mask *= 2
    rest = swap(total, snap)
    return jnp.where(core == 0, jnp.concatenate([total, rest]), jnp.concatenate([rest, total]))


def on_device(snapshots, block_starts, point_slab, slab_weight):
    dft_table, row_sums = make_tables(WIN, NF)
    parts = lax.axis_size("snap")
    send = pack(jnp.transpose(snapshots, (1, 0, 2)), parts)
    series = lax.all_to_all(send, "snap", split_axis=0, concat_axis=0, tiled=True)
    tables = shifted_tables(block_starts, dft_table)
    comps, points = (series.shape[1], series.shape[3])
    slab_ids = jnp.arange(slab_weight.shape[0], dtype=jnp.int32)
    chosen = jnp.where(point_slab[:, None] == slab_ids[None, :], slab_weight[None, :], 0.0)
    root_weight = jnp.sqrt(jnp.sum(chosen, axis=1) / (0.375 * WIN))
    sums = jnp.transpose(row_sums).reshape(2 * NF)
    amplitude, gram = spectra_and_gram(sums, tables, series, root_weight[None, :])
    all_points = points * lax.axis_size("pts") * lax.axis_size("snap")
    total = sum_everywhere(gram.reshape(GROUPS * PAD, 128)).reshape(GROUPS, PAD, 128)
    weights, upper = factor(total, 1.0 / (comps * all_points))
    mode_field = jnp.transpose(project(weights, amplitude), (3, 0, 1, 2, 4))
    upper = jnp.transpose(upper.reshape(2, GROUPS, PAD, PACK, PAD), (0, 1, 3, 2, 4))
    r_factor = upper.reshape(2, GROUPS * PACK, PAD, PAD)[:, :NF, :NB, :NB]
    return (mode_field, r_factor)


def solution(mesh):
    in_specs = (P("snap", None, "pts"), P(), P(("pts", "snap")), P())
    out_specs = (P(None, None, None, None, ("pts", "snap")), P())
    return jax.shard_map(
        on_device, mesh=mesh, in_specs=in_specs, out_specs=out_specs, check_vma=False
    )
```
